32 devices in a mesh: row: 4 (over x, core), col: 2 (over y), grp: 4 (over z).
Axes of the slice: x: 2, y: 2, z: 4, core: 2. Of those that a mesh axis runs over, the one named last changes fastest.
Arguments:
- amplitudes: bfloat16 [512, 8, 1024], P(None, 'row', ('col', 'grp')), may hold values from -6 to 6
- ladder_integrals: bfloat16 [8, 1024, 16, 1024], P('row', None, 'grp', 'col'), may hold values from -0.0625 to 0.0625
- cycle_integrals: bfloat16 [16, 16, 16, 16], replicated, may hold values from -0.375 to 0.375
- pair_list: int32 [512, 2], replicated, may hold values from 0 to 127, as said below
- occ_energy: float32 [128], replicated, may hold values from -3 to -0.5
- batch_energy: float32 [16], replicated, may hold values from 0.2 to 4
- virt_energy: float32 [1024], P('col'), may hold values from 0.2 to 4
Outputs:
- update: float32 [16, 16, 32, 1024], P('row', None, 'grp', 'col')
The draws below stay inside these ranges and needn't reach their ends.
Inputs may be any that keep to these rules, and one draw needn't show every extreme that they name: `pair_list`: pair p holds the occupied orbital of window row p // 32 and that of window column p % 32; the 16 row orbitals and 32 column orbitals are all distinct.
All inputs are finite; a program needn't handle non-finite values.
Results may differ from the reference program's by a relative error of at most 0.0029.
Values may be sent and summed in bfloat16 or wider, within the bound.
No kernel may reach another device: no remote copies, remote signals or barrier semaphores. Data moves between devices by JAX's collectives and lax.ppermute only.
A program may use at most 64 MiB of HBM per device.

```python
import jax
import jax.numpy as jnp
from jax import lax

NVIRT = 1024
NOCC = 128
OCC_I = 16
OCC_J = 32
NPAIR = 512
CBATCH = 8
ABATCH = 16


def draw_pair_list(key, part):
    order = jax.random.permutation(jax.random.fold_in(key, 7), NOCC).astype(jnp.int32)
    row_orbitals = order[:OCC_I]
    col_orbitals = order[OCC_I:OCC_I + OCC_J]
    first = jnp.broadcast_to(row_orbitals[:, None], (OCC_I, OCC_J))
    second = jnp.broadcast_to(col_orbitals[None, :], (OCC_I, OCC_J))
    return jnp.stack([first, second], axis=-1).reshape(OCC_I * OCC_J, 2).astype(jnp.int32)


def block_scale(own_key, dims, pieces, low, high):
    gain = 1.0
    for dim, blocks in pieces:
        draws = jax.random.uniform(jax.random.fold_in(jax.random.fold_in(own_key, 6), dim), (blocks,), jnp.float32, low / len(pieces), high / len(pieces))
        gain = gain * jnp.repeat(jnp.exp(draws), dims[dim] // blocks).reshape((-1,) + (1,) * (len(dims) - 1 - dim))
    return gain


def centred(stream_key, shape, spread, limit, cuts=(), dtype=jnp.bfloat16):
    result = spread * jax.random.normal(stream_key, shape, jnp.float32)
    if cuts:
        result = result * block_scale(stream_key, shape, cuts, -0.22, 0.18)
    return jnp.clip(result, -limit, limit).astype(dtype)


def setup_inputs(seed: int = 0) -> dict:
    seeds = jax.random.split(jax.random.key(seed), 8)
    amplitudes = centred(seeds[0], (NPAIR, CBATCH, NVIRT), 1.0, 6.0, ((1, 4), (2, 8)))
    ladder_integrals = centred(seeds[1], (CBATCH, NVIRT, ABATCH, NVIRT), (CBATCH * NVIRT) ** -0.5, 0.0625, ((0, 4), (2, 4), (3, 2)))
    cycle_integrals = centred(seeds[2], (OCC_I, ABATCH, OCC_I, ABATCH), (OCC_I * ABATCH) ** -0.5, 0.375)
    pair_list = draw_pair_list(jax.random.fold_in(seeds[7], 71), 0)
    occ_energy = jnp.clip(jax.random.uniform(seeds[4], (NOCC,), jnp.float32, -3.0, -0.5), -3.0, -0.5)
    batch_energy = jnp.clip(jax.random.uniform(seeds[5], (ABATCH,), jnp.float32, 0.2, 4.0), 0.2, 4.0)
    virt_energy = jnp.clip(0.2 + 3.8 * jax.random.uniform(seeds[6], (NVIRT,), jnp.float32) ** block_scale(seeds[6], (NVIRT,), ((0, 2),), -0.2, 0.2), 0.2, 4.0)
    return {"amplitudes": amplitudes, "ladder_integrals": ladder_integrals, "cycle_integrals": cycle_integrals, "pair_list": pair_list, "occ_energy": occ_energy, "batch_energy": batch_energy, "virt_energy": virt_energy}


def reference(amplitudes, ladder_integrals, cycle_integrals, pair_list, occ_energy, batch_energy, virt_energy):
    def ladder_step(total, inputs):
        amp_slab, integral_slab = inputs
        flat = integral_slab.reshape(NVIRT, ABATCH * NVIRT)
        return total + jnp.dot(amp_slab, flat, preferred_element_type=jnp.float32), None

    start = jnp.zeros((NPAIR, ABATCH * NVIRT), jnp.float32)
    summed, unused = lax.scan(ladder_step, start, (jnp.transpose(amplitudes, (1, 0, 2)), ladder_integrals))
    ladder = summed.astype(jnp.bfloat16).reshape(OCC_I, OCC_J, ABATCH, NVIRT)
    regrouped = jnp.transpose(ladder, (0, 2, 1, 3))
    cycle = jnp.einsum("iakc,kcjb->iajb", cycle_integrals.astype(jnp.float32), regrouped.astype(jnp.float32))
    pair_grid = pair_list.reshape(OCC_I, OCC_J, 2)
    pair_energy = occ_energy[pair_grid[:, :, 0]] + occ_energy[pair_grid[:, :, 1]]
    denom = pair_energy[:, None, :, None] - batch_energy[None, :, None, None] - virt_energy[None, None, None, :]
    return (regrouped.astype(jnp.float32) + cycle) / denom
```

```python
import functools

import jax
import jax.numpy as jnp
from jax import lax
from jax.experimental import pallas as pl
from jax.experimental.pallas import tpu as pltpu
from jax.sharding import PartitionSpec as P

OCC_I = 16
OCC_J = 32
CHUNKS = 2
F32 = jnp.float32
BF16 = jnp.bfloat16


def pair_energies(pair_list, occ_energy, occ_rows, occ_cols):
    row_index = lax.axis_index("row")
    grp_index = lax.axis_index("grp")
    pair_grid = pair_list.reshape(OCC_I, OCC_J, 2)
    mine = lax.dynamic_slice_in_dim(pair_grid, row_index * occ_rows, occ_rows, 0)
    mine = lax.dynamic_slice_in_dim(mine, grp_index * occ_cols, occ_cols, 1)
    orbital_ids = lax.broadcasted_iota(jnp.int32, (1, 1, 1, occ_energy.shape[0]), 3)
    looked = jnp.sum(jnp.where(mine[:, :, :, None] == orbital_ids, occ_energy, 0.0), axis=-1)
    return looked[:, :, 0] + looked[:, :, 1]


def general(
    amplitudes, ladder_integrals, cycle_integrals, pair_list, occ_energy, batch_energy, virt_energy
):
    cont_here, virt_all, batch_here, virt_here = ladder_integrals.shape
    occ_rows = OCC_I // lax.axis_size("row")
    occ_cols = OCC_J // lax.axis_size("grp")
    row_index = lax.axis_index("row")
    flat_ladder = ladder_integrals.reshape(cont_here, virt_all, batch_here * virt_here)
    partial_value = jnp.einsum(
        "pcd,cdx->px",
        lax.all_gather(amplitudes, ("col", "grp"), axis=2, tiled=True),
        flat_ladder,
        preferred_element_type=F32,
    )
    summed = lax.psum_scatter(partial_value, "row", scatter_dimension=0, tiled=True)
    ladder_part = summed.astype(BF16).reshape(occ_rows, OCC_J, batch_here, virt_here)
    regrouped = lax.all_to_all(ladder_part, "grp", split_axis=1, concat_axis=2, tiled=True)
    row_block = lax.dynamic_slice_in_dim(cycle_integrals, row_index * occ_rows, occ_rows, 0)
    cycle = jnp.einsum(
        "iakc,kjcb->iajb",
        row_block,
        lax.all_gather(regrouped, "row", axis=0, tiled=True),
        preferred_element_type=F32,
    )
    ladder_term = jnp.transpose(regrouped, (0, 2, 1, 3)).astype(F32)
    pair_energy = pair_energies(pair_list, occ_energy, occ_rows, occ_cols)
    denom = (
        pair_energy[:, None, :, None]
        - batch_energy[None, :, None, None]
        - virt_energy[None, None, None, :]
    )
    return (ladder_term + cycle) / denom


VM = pl.BlockSpec(memory_space=pltpu.VMEM)
SM = pl.BlockSpec(memory_space=pltpu.SMEM)


def block_dot(idx_ref, slots, blocks, b_refs, a, rows, cols, depth):
    total = None
    for slot, block in zip(slots, blocks):
        start = pl.multiple_of(idx_ref[slot] * depth, depth)
        lhs = jnp.concatenate([block[c, rows, :] for c in range(len(b_refs))], axis=1)
        rhs = jnp.concatenate([b[a, pl.ds(start, depth), cols] for b in b_refs], axis=0)
        part = jnp.dot(lhs, rhs, preferred_element_type=F32)
        total = part if total is None else total + part
    return total


def stage_kernel(slots, n_cont, has_acc, idx_ref, *refs):
    blocks = refs[: len(slots)]
    b_refs = refs[len(slots) : len(slots) + n_cont]
    acc_ref = refs[len(slots) + n_cont] if has_acc else None
    out_ref = refs[-1]
    depth = blocks[0].shape[2]
    half = blocks[0].shape[1] // 2

    @pl.loop(0, out_ref.shape[0])
    def _(a):
        for h in range(2):
            rows = pl.ds(h * half, half)
            part = block_dot(idx_ref, slots, blocks, b_refs, a, rows, slice(None), depth)
            if has_acc:
                part = part + acc_ref[a, rows, :]
            out_ref[a, rows, :] = part


def stage(idx, slots, blocks, bs, acc):
    n_a, _, n_b = bs[0].shape
    rows = blocks[0].shape[1]
    operands = (idx, *blocks, *bs) + (() if acc is None else (acc,))
    return pl.pallas_call(
        functools.partial(stage_kernel, slots, len(bs), acc is not None),
        out_shape=jax.ShapeDtypeStruct((n_a, rows, n_b), F32),
        in_specs=[SM] + [VM] * (len(operands) - 1),
        out_specs=VM,
        name="stage",
    )(*operands)


def last_kernel(slots, n_cont, chunk, rows_here, idx_ref, *refs):
    blocks = refs[: len(slots)]
    b_refs = refs[len(slots) : len(slots) + n_cont]
    acc_ref, keep_ref, send_ref = refs[-3:]
    depth = blocks[0].shape[2]
    half = keep_ref.shape[2]
    core = idx_ref[idx_ref.shape[0] - 1]
    rows = pl.ds(chunk * rows_here, rows_here)

    @pl.loop(0, keep_ref.shape[0])
    def _(a):
        for ref, which in ((send_ref, 1 - core), (keep_ref, core)):
            cols = pl.ds(pl.multiple_of(which * half, half), half)
            part = block_dot(idx_ref, slots, blocks, b_refs, a, rows, cols, depth)
            ref[a] = part + acc_ref[a, rows, cols]


def last_stage(idx, slots, blocks, bs, acc, chunk, chunks):
    n_a, rows, n_b = acc.shape
    rows_here = rows // chunks
    shape = jax.ShapeDtypeStruct((n_a, rows_here, n_b // 2), F32)
    operands = (idx, *blocks, *bs, acc)
    return pl.pallas_call(
        functools.partial(last_kernel, slots, len(bs), chunk, rows_here),
        out_shape=(shape, shape),
        in_specs=[SM] + [VM] * (len(operands) - 1),
        out_specs=(VM, VM),
        name="last_stage",
    )(*operands)


def final_kernel(chunks, srcs, quarter_ref, mat_ref, pe_ref, virt_ref, *refs):
    parts = refs[: chunks * srcs]
    out_ref, buf_ref, sem_ref = refs[-3:]
    n_i, n_a, n_j, _ = buf_ref.shape[1:]
    rows = n_i * n_a
    lanes = buf_ref.shape[4]
    j_per = n_j // chunks
    mat = mat_ref[...]
    copies = []
    for src in range(srcs):
        quarter = quarter_ref[src]
        start = pl.multiple_of(quarter * lanes, lanes)
        virt = virt_ref[:, pl.ds(start, lanes)]
        for chunk in range(chunks):
            part = parts[chunk * srcs + src]
            step = part.shape[2] // j_per
            for jj in range(j_per):
                j = chunk * j_per + jj
                tile = part[:, :, pl.ds(jj * step, step), :]
                rhs = tile.reshape(-1, lanes)
                both = jnp.dot(mat, rhs, preferred_element_type=F32)
                denom = pe_ref[:, j : j + 1] - virt
                value = (both[:rows] + both[rows:]) / denom
                buf_ref[src, :, :, j, :] = value.reshape(n_i, n_a, lanes)
        copy = pltpu.make_async_copy(
            buf_ref.at[src], out_ref.at[:, :, :, pl.ds(start, lanes)], sem_ref.at[src]
        )
        copy.start()
        copies.append(copy)
    for copy in copies:
        copy.wait()


def final(quarters, mat, pe, virt, parts, chunks, out_shape):
    srcs = len(parts) // chunks
    n_i, n_a, n_j, n_b = out_shape
    lanes = n_b // srcs
    return pl.pallas_call(
        functools.partial(final_kernel, chunks, srcs),
        out_shape=jax.ShapeDtypeStruct(out_shape, F32),
        in_specs=[SM] + [VM] * (3 + len(parts)),
        out_specs=pl.BlockSpec(memory_space=pl.ANY),
        scratch_shapes=[
            pltpu.VMEM((srcs, n_i, n_a, n_j, lanes), F32),
            pltpu.SemaphoreType.DMA((srcs,)),
        ],
        name="final",
    )(quarters, mat, pe, virt, *parts)


def tuned(
    amplitudes, ladder_integrals, cycle_integrals, pair_list, occ_energy, batch_energy, virt_energy
):
    rows, cols, grps = (lax.axis_size(name) for name in ("row", "col", "grp"))
    cont_here, virt_all, batch_here, virt_here = ladder_integrals.shape
    depth = amplitudes.shape[2]
    occ_rows, occ_cols = OCC_I // rows, OCC_J // grps
    row, col, grp = (lax.axis_index(name) for name in ("row", "col", "grp"))
    x, core = row // 2, row % 2
    chunks = CHUNKS
    j_per = occ_cols // chunks

    core_swap = [(r, r ^ 1) for r in range(rows)]
    x_swap = [(r, (r + 2) % rows) for r in range(rows)]
    y_swap = [(c, (c + 1) % cols) for c in range(cols)]

    def over_y(v):
        return lax.ppermute(v, "col", y_swap)

    own = amplitudes.reshape(OCC_I, grps, chunks, j_per, cont_here, depth)
    own = jnp.transpose(own, (4, 2, 1, 3, 0, 5)).reshape(cont_here, OCC_I * OCC_J, depth)
    bs = [jnp.transpose(ladder_integrals[c], (1, 0, 2)) for c in range(cont_here)]

    up = lax.ppermute(own, "grp", [(g, g + 1) for g in range(grps - 1)])
    down = lax.ppermute(own, "grp", [(g + 1, g) for g in range(grps - 1)])
    own_y = over_y(own)
    last = grp == grps - 1
    near = jnp.where(last, up, down)
    up2 = lax.ppermute(up, "grp", [(g, g + 1) for g in range(1, grps - 1)])
    down2 = lax.ppermute(down, "grp", [(g + 1, g) for g in range(grps - 2)])
    near_y = over_y(near)
    upper = grp >= 2
    mid = jnp.where(upper, up2, down2)
    far3 = lax.ppermute(mid, "grp", [(2, 3), (1, 0)])
    mid_y = over_y(mid)
    inner = (grp == 1) | (grp == 2)
    far = jnp.where(inner, up, far3)
    far_y = over_y(far)

    z_near = jnp.where(last, grp - 1, grp + 1)
    z_mid = jnp.where(upper, grp - 2, grp + 2)
    z_far = jnp.where(inner, grp - 1, grps - 1 - grp)
    here, there = col * grps, (cols - 1 - col) * grps
    zs = (grp, z_near, z_mid, z_far)
    idx = jnp.stack([here + z for z in zs] + [there + z for z in zs] + [core]).astype(jnp.int32)
    acc = stage(idx, (0, 4, 1, 2, 5), (own, own_y, near, mid, near_y), bs, None)
    acc = stage(idx, (6, 3), (mid_y, far), bs, acc)

    rows_here = acc.shape[1] // chunks
    lanes = virt_here // rows
    parts = []
    for chunk in range(chunks):
        keep, send = last_stage(idx, (7,), (far_y,), bs, acc, chunk, chunks)
        got = lax.ppermute(send, "row", core_swap)
        keep_x = keep.reshape(batch_here, rows_here, 2, lanes)
        got_x = got.reshape(batch_here, rows_here, 2, lanes)
        keep_x = keep.reshape(batch_here, rows_here, 2 * lanes)
        got_x = got

        def half(v, which):
            return lax.dynamic_slice_in_dim(v, which * lanes, lanes, 2)

        theirs = (half(keep_x, 1 - x) + half(got_x, 1 - x)).astype(BF16)
        from_x = lax.ppermute(theirs, "row", x_swap)
        mine = half(keep_x, x) + half(got_x, x) + from_x.astype(F32)
        mine = mine.astype(BF16).reshape(batch_here, grps, rows_here // grps, lanes)
        mine = jnp.transpose(mine, (1, 0, 2, 3))
        got_z = [lax.dynamic_slice_in_dim(mine, grp, 1, 0)]
        for s in range(1, grps):
            block = lax.dynamic_slice_in_dim(mine, (grp + s) % grps, 1, 0)
            got_z.append(lax.ppermute(block, "grp", [(g, (g + s) % grps) for g in range(grps)]))
        w = jnp.concatenate(got_z, 0)
        w_x = lax.ppermute(w, "row", x_swap)
        w_c = lax.ppermute(w, "row", core_swap)
        w_xc = lax.ppermute(w_x, "row", core_swap)
        parts += [w, w_c, w_x, w_xc]

    quarters = jnp.stack(
        [core * 2 + x, (1 - core) * 2 + x, core * 2 + 1 - x, (1 - core) * 2 + 1 - x]
    ).astype(jnp.int32)
    row_block = lax.dynamic_slice_in_dim(cycle_integrals, row * occ_rows, occ_rows, 0)
    n_a = batch_here * grps
    row_block = row_block.reshape(occ_rows, n_a, OCC_I, grps, batch_here)
    order = (grp - jnp.arange(grps)) % grps
    pick = (order[:, None] == jnp.arange(grps)[None, :]).astype(BF16)
    mat = jnp.einsum("iakzc,sz->iasck", row_block, pick, preferred_element_type=F32).astype(BF16)
    mat = mat.reshape(occ_rows * n_a, n_a * OCC_I)
    i_ids = row * occ_rows + jnp.arange(occ_rows)
    same_i = i_ids[:, None] == jnp.arange(OCC_I)[None, :]
    src_a = (order[:, None] * batch_here + jnp.arange(batch_here)[None, :]).reshape(-1)
    same_a = jnp.arange(n_a)[:, None] == src_a[None, :]
    unit = same_i[:, None, None, :] & same_a[None, :, :, None]
    unit = unit.astype(BF16).reshape(occ_rows * n_a, n_a * OCC_I)
    both = jnp.concatenate([mat, unit], 0)

    pair_energy = pair_energies(pair_list, occ_energy, occ_rows, occ_cols)
    pe = pair_energy[:, None, :] - batch_energy[None, :, None]
    pe = pe.reshape(occ_rows * n_a, occ_cols)
    return final(
        quarters, both, pe, virt_energy.reshape(1, -1), parts, chunks,
        (occ_rows, n_a, occ_cols, virt_here),
    )


def fits(mesh):
    sizes = dict(mesh.shape)
    return sizes["row"] == 4 and sizes["col"] == 2 and sizes["grp"] == 4


def solution(mesh):
    placed = (
        P(None, "row", ("col", "grp")),
        P("row", None, "grp", "col"),
        P(),
        P(),
        P(),
        P(),
        P("col"),
    )
    return jax.shard_map(
        tuned if fits(mesh) else general,
        mesh=mesh,
        in_specs=placed,
        out_specs=P("row", None, "grp", "col"),
        check_vma=False,
    )
```
